32 devices in a mesh: order: 1, shard: 32 (over z, y, x, core).
Axes of the slice: x: 2, y: 2, z: 4, core: 2. Of those that a mesh axis runs over, the one named last changes fastest.
Arguments:
- sky_coeffs: float32 [32, 2, 2048], P('shard'), may hold values from -6 to 6
- beam_coeffs: float32 [64, 2048], P('order'), may hold values from -0.09375 to 0.09375
- wigner: bfloat16 [32, 64, 2048, 128], P('shard', 'order'), may hold values from -0.125 to 0.125
- visits: int32 [32, 32, 4], P(('order', 'shard')), may hold values from -1 to 511, as said below
- point_slot: int32 [524288], P(('order', 'shard')), may hold values from 0 to 127, as said below
- phi_cell: int32 [524288], P(('order', 'shard')), may hold values from 0 to 30
- psi_cell: int32 [524288], P(('order', 'shard')), may hold values from 0 to 127
- fraction: float32 [2, 524288], P(None, ('order', 'shard')), may hold values from 0 to 1
Outputs:
- timeline: float32 [524288], P(('order', 'shard'))
The draws below stay inside these ranges and needn't reach their ends.
Inputs may be any that keep to these rules, and one draw needn't show every extreme that they name: Live entries of one row visits[r, d] are distinct tiles of owner d and come first; every row holds 1 to 4 live entries; for every device r some owner d has all 4 entries live. `point_slot`: every pointing names a live entry of its own device's visit list. Of one device's pointings, exactly 768 name each of half of the owners and 256 each of the others.
All inputs are finite; a program needn't handle non-finite values.
Results may differ from the reference program's by a relative error of at most 0.008.
Values may be sent and summed in bfloat16 or wider, within the bound.
A program may use at most 128 MiB of HBM per device.

```python
import math
import jax
import jax.numpy as jnp
from jax import lax

L = 2048
KBEAM = 64
NPHI = 4096
NPSI = 128
PHI_T = 32
SLOTS = 4
ROWS = 4
P_DEV = 16384
MTOT = 32
THETA = 128
PTOT = 524288
BLOCKS = 128
TPO = 512
N_ORDER = 1
N_SHARD = 32
DEVICES = 32


def visit_plan(key):
    base = jax.random.fold_in(key, 7)
    key_count, key_score, key_full = jax.random.split(base, 3)
    counts = jax.random.randint(key_count, (DEVICES, DEVICES), 1, SLOTS + 1)
    full_owner = jax.random.permutation(key_full, DEVICES)
    owners = jnp.arange(DEVICES, dtype=jnp.int32)[None, :]
    counts = jnp.where(owners == full_owner[:, None], SLOTS, counts)
    scores = jax.random.randint(key_score, (DEVICES, DEVICES, TPO), 0, 1048576) * TPO
    scores = scores + jnp.arange(TPO, dtype=jnp.int32)[None, None, :]
    picked = jnp.argsort(scores, axis=-1)[:, :, :SLOTS].astype(jnp.int32)
    live = jnp.arange(SLOTS, dtype=jnp.int32)[None, None, :] < counts[:, :, None]
    return (jnp.where(live, picked, -1).astype(jnp.int32), counts.astype(jnp.int32))


def draw_visits(key, part):
    table, counts = visit_plan(key)
    return table


def draw_point_slot(key, part):
    table, counts = visit_plan(key)
    key_perm, key_order, key_slot = jax.random.split(jax.random.fold_in(key, 11), 3)
    per_owner = P_DEV // DEVICES
    half = P_DEV // 2
    position = jnp.arange(P_DEV, dtype=jnp.int32)
    light = position % DEVICES
    heavy = (position - half) // per_owner
    rank_owner = jnp.where(position < half, light, heavy).astype(jnp.int32)
    perm_scores = jax.random.randint(key_perm, (DEVICES, DEVICES), 0, 65536) * DEVICES
    perm_scores = perm_scores + jnp.arange(DEVICES, dtype=jnp.int32)[None, :]
    owner_perm = jnp.argsort(perm_scores, axis=-1).astype(jnp.int32)
    owner_base = owner_perm[:, rank_owner]
    order_scores = jax.random.randint(key_order, (DEVICES, P_DEV), 0, 8192) * P_DEV
    order_scores = order_scores + position[None, :]
    shuffle = jnp.argsort(order_scores, axis=-1).astype(jnp.int32)
    owner = jnp.take_along_axis(owner_base, shuffle, axis=1).reshape(PTOT).astype(jnp.int32)
    device = jnp.arange(PTOT, dtype=jnp.int32) // P_DEV
    live_count = counts[device, owner]
    slot = jax.random.randint(key_slot, (PTOT,), 0, 65536) * live_count // 65536
    return (owner * SLOTS + slot).astype(jnp.int32)


def touch_ends(result, stream_key, least, top_value):
    place = [jax.random.randint(jax.random.fold_in(stream_key, axis), (), 0, length) for axis, length in enumerate(result.shape)]
    longest = result.shape.index(max(result.shape))
    next_to = place[:longest] + [(place[longest] + 1) % result.shape[longest]] + place[longest + 1:]
    return result.at[tuple(place)].set(least).at[tuple(next_to)].set(top_value)


def shard_levels(key, extent, shards, low, high):
    loudness = 1.0
    for axis_at, parts in shards:
        steps = jax.random.uniform(jax.random.fold_in(jax.random.fold_in(key, 6), axis_at), (parts,), jnp.float32, low / len(shards), high / len(shards))
        loudness = loudness * jnp.repeat(jnp.exp(steps), extent[axis_at] // parts).reshape((-1,) + (1,) * (len(extent) - 1 - axis_at))
    return loudness


def bell_draw(rng, dims, width, limit, shards=(), kind=jnp.bfloat16):
    result = width * jax.random.normal(rng, dims, jnp.float32)
    if shards:
        result = result * shard_levels(rng, dims, shards, -0.22, 0.18)
    return jnp.clip(result, -limit, limit).astype(kind)


def setup_inputs(seed: int = 0) -> dict:
    splits = jax.random.split(jax.random.key(seed), 9)
    sky_coeffs = bell_draw(splits[0], (MTOT, 2, L), 1.0, 6.0, ((0, 32),), jnp.float32)
    beam_coeffs = bell_draw(splits[1], (KBEAM, L), (2 * MTOT * KBEAM) ** -0.5, 0.09375, (), jnp.float32)
    wigner = bell_draw(splits[2], (MTOT, KBEAM, L, THETA), L ** -0.5, 0.125, ((0, 32),))
    visits = draw_visits(jax.random.fold_in(splits[8], 71), 0)
    point_slot = draw_point_slot(jax.random.fold_in(splits[8], 71), 0)
    phi_cell = touch_ends(jax.random.randint(splits[5], (PTOT,), 0, PHI_T - 1), jax.random.fold_in(splits[5], 1), 0, (PHI_T - 1) - 1).astype(jnp.int32)
    psi_cell = touch_ends(jax.random.randint(splits[6], (PTOT,), 0, NPSI), jax.random.fold_in(splits[6], 1), 0, NPSI - 1).astype(jnp.int32)
    fraction = jnp.clip(1.0 * jax.random.uniform(splits[7], (2, PTOT), jnp.float32) ** shard_levels(splits[7], (2, PTOT), ((1, 32),), -0.2, 0.2), 0.0, 1.0)
    return {"sky_coeffs": sky_coeffs, "beam_coeffs": beam_coeffs, "wigner": wigner, "visits": visits, "point_slot": point_slot, "phi_cell": phi_cell, "psi_cell": psi_cell, "fraction": fraction}


def wave_table(count, modes, first):
    grid = jnp.arange(count, dtype=jnp.int32)[:, None]
    mode = jnp.arange(modes, dtype=jnp.int32)[None, :] + first
    phase = ((grid * mode) % count).astype(jnp.float32) * (2.0 * math.pi / count)
    return jnp.cos(phase).astype(jnp.bfloat16), jnp.sin(phase).astype(jnp.bfloat16)


def reference(sky_coeffs, beam_coeffs, wigner, visits, point_slot, phi_cell, psi_cell, fraction):
    def mode_terms(pair):
        sky_mode, table_mode = pair
        weighted = (sky_mode[None, :, :] * beam_coeffs[:, None, :]).astype(jnp.bfloat16)
        terms = jnp.einsum("kcl,klt->tkc", weighted.astype(jnp.float32), table_mode.astype(jnp.float32))
        return terms.astype(jnp.bfloat16)

    coeffs = lax.map(mode_terms, (sky_coeffs, wigner))
    coeffs = jnp.transpose(coeffs, (1, 0, 2, 3))
    cos_phi, sin_phi = wave_table(NPHI, MTOT, 0)
    cos_psi, sin_psi = wave_table(NPSI, KBEAM, 0)
    group_orders = KBEAM // N_ORDER
    cos_group = jnp.transpose(cos_psi).reshape(N_ORDER, group_orders, NPSI).astype(jnp.float32)
    sin_group = jnp.transpose(sin_psi).reshape(N_ORDER, group_orders, NPSI).astype(jnp.float32)

    def theta_row(row):
        real_part = row[:, :, 0]
        imag_part = row[:, :, 1]
        synth_real = (jnp.dot(cos_phi, real_part, preferred_element_type=jnp.float32)
                      - jnp.dot(sin_phi, imag_part, preferred_element_type=jnp.float32)).astype(jnp.bfloat16)
        synth_imag = (jnp.dot(sin_phi, real_part, preferred_element_type=jnp.float32)
                      + jnp.dot(cos_phi, imag_part, preferred_element_type=jnp.float32)).astype(jnp.bfloat16)
        grouped_real = synth_real.reshape(NPHI, N_ORDER, group_orders).astype(jnp.float32)
        grouped_imag = synth_imag.reshape(NPHI, N_ORDER, group_orders).astype(jnp.float32)
        partial_value = (jnp.einsum("pok,okq->opq", grouped_real, cos_group)
                   - jnp.einsum("pok,okq->opq", grouped_imag, sin_group))
        rounded = lax.optimization_barrier(partial_value.astype(jnp.bfloat16)).astype(jnp.float32)
        return jnp.sum(rounded, axis=0).astype(jnp.bfloat16)

    cube = lax.map(theta_row, coeffs)
    flat_cube = cube.reshape(-1)
    device = (jnp.arange(PTOT, dtype=jnp.int32) // P_DEV).astype(jnp.int32)
    owner = point_slot // SLOTS
    tile = visits[device, owner, point_slot % SLOTS]
    owner_order = owner // N_SHARD
    owner_shard = owner % N_SHARD
    row_index = owner_shard * ROWS + tile // BLOCKS
    phi_index = owner_order * (NPHI // N_ORDER) + (tile % BLOCKS) * PHI_T + phi_cell
    next_psi = (psi_cell + 1) % NPSI
    base = row_index * (NPHI * NPSI) + phi_index * NPSI
    corner_aa = flat_cube[base + psi_cell].astype(jnp.float32)
    corner_ab = flat_cube[base + next_psi].astype(jnp.float32)
    corner_ba = flat_cube[base + NPSI + psi_cell].astype(jnp.float32)
    corner_bb = flat_cube[base + NPSI + next_psi].astype(jnp.float32)
    along_phi = fraction[0]
    along_psi = fraction[1]
    return ((1.0 - along_phi) * ((1.0 - along_psi) * corner_aa + along_psi * corner_ab)
            + along_phi * ((1.0 - along_psi) * corner_ba + along_psi * corner_bb))
```

```python
import functools
import math

import jax
import jax.numpy as jnp
from jax import lax
from jax.experimental import pallas as pl
from jax.experimental.pallas import tpu as pltpu
from jax.sharding import PartitionSpec as P

NPHI = 4096
NPSI = 128
PHI_T = 32
LOW = 8
LANES = 128
CHUNK = 256


def wave_table(count, grid, mode):
    phase = ((grid * mode) % count).astype(jnp.float32) * (2.0 * math.pi / count)
    return jnp.cos(phase), jnp.sin(phase)


def interpolate(
    modes,
    orders,
    coeffs_ref,
    row_ref,
    turn_cos_ref,
    turn_sin_ref,
    phi_table_ref,
    psi_table_ref,
    slot_ref,
    phi_ref,
    psi_ref,
    fraction_ref,
    out_ref,
    picked,
    edge,
    synth,
    wave,
):
    terms = 2 * orders
    high = PHI_T // LOW
    theta, slots = coeffs_ref.shape[1], row_ref.shape[1]
    groups = slots // LANES
    for g in range(groups):
        lanes = slice(g * LANES, (g + 1) * LANES)
        chosen = (
            lax.broadcasted_iota(jnp.int32, (theta, LANES), 0) == row_ref[:, lanes]
        ).astype(jnp.float32).astype(jnp.bfloat16)

        def pick(m, carry):
            rows = pl.ds(pl.multiple_of(m * 4 * terms, 4 * terms), 4 * terms)
            picked[rows, :] = jnp.dot(
                coeffs_ref[rows, :], chosen, preferred_element_type=jnp.float32
            )
            return carry

        lax.fori_loop(0, modes // 4, pick, 0)
        turn_cos, turn_sin = turn_cos_ref[:, lanes], turn_sin_ref[:, lanes]

        def sum_modes(k, carry):
            real = picked[pl.ds(2 * k, modes, stride=terms), :]
            imag = picked[pl.ds(2 * k + 1, modes, stride=terms), :]
            turned = jnp.concatenate(
                [turn_cos * real - turn_sin * imag, turn_sin * real + turn_cos * imag], axis=0
            ).astype(jnp.bfloat16)
            values = jnp.dot(phi_table_ref[...], turned, preferred_element_type=jnp.float32)
            for h in range(high):
                synth[
                    pl.ds(pl.multiple_of(k * 2 * LOW, 2 * LOW), 2 * LOW),
                    h * slots + g * LANES : h * slots + (g + 1) * LANES,
                ] = values[h * 2 * LOW : (h + 1) * 2 * LOW].astype(jnp.bfloat16)
            edge[pl.ds(pl.multiple_of(k * 2 * high, 2 * high), 2 * high), :] = values[
                2 * PHI_T :
            ]
            return carry

        lax.fori_loop(0, orders, sum_modes, 0, unroll=4)
        for part in range(2):
            for h in range(high):
                synth[
                    terms * LOW + part * orders : terms * LOW + (part + 1) * orders,
                    h * slots + g * LANES : h * slots + (g + 1) * LANES,
                ] = edge[pl.ds(part * high + h, orders, stride=2 * high), :].astype(jnp.bfloat16)

    def chunk(i, carry):
        phi, psi = phi_ref[i], psi_ref[i]
        along = fraction_ref[i]
        along_phi, along_psi = along[0:1], along[1:2]
        key = (phi // LOW) * slots + slot_ref[i]
        entry = (
            lax.broadcasted_iota(jnp.int32, (high * slots, CHUNK), 0) == key
        ).astype(jnp.float32).astype(jnp.bfloat16)
        at_psi = lax.broadcasted_iota(jnp.int32, (NPSI, CHUNK), 0)
        weight = jnp.where(
            at_psi == psi, 1.0 - along_psi, jnp.where(at_psi == (psi + 1) % NPSI, along_psi, 0.0)
        )
        coarse = weight.astype(jnp.bfloat16)
        fine = (weight - coarse.astype(jnp.float32)).astype(jnp.bfloat16)
        waves = jnp.dot(
            psi_table_ref[...],
            jnp.concatenate([coarse, fine], axis=0),
            preferred_element_type=jnp.float32,
        )
        wave[...] = waves
        values = jnp.dot(synth[...], entry, preferred_element_type=jnp.float32)
        sums = [jnp.zeros((LOW, CHUNK), jnp.float32) for _ in range(4)]
        for k in range(orders):
            for part in range(2):
                at = (2 * k + part) * LOW
                line = part * orders + k
                sums[at // LOW % 4] += values[at : at + LOW] * wave[line : line + 1, :]
        inner = (sums[0] + sums[1]) + (sums[2] + sums[3])
        last = jnp.sum(values[terms * LOW :] * waves, axis=0, keepdims=True)
        low = phi % LOW
        at_low = lax.broadcasted_iota(jnp.int32, (LOW, CHUNK), 0)
        weight_phi = jnp.where(
            at_low == low, 1.0 - along_phi, jnp.where(at_low == low + 1, along_phi, 0.0)
        )
        total = jnp.sum(inner * weight_phi, axis=0, keepdims=True)
        out_ref[i] = total + jnp.where(low == LOW - 1, along_phi, 0.0) * last
        return carry

    lax.fori_loop(0, slot_ref.shape[0], chunk, 0)


def phi_rows(modes):
    mode = jnp.arange(modes, dtype=jnp.int32)[None, :]
    high = PHI_T // LOW
    cos, sin = wave_table(NPHI, jnp.arange(PHI_T, dtype=jnp.int32)[:, None], mode)
    real = jnp.concatenate([cos, -sin], axis=1)
    imag = jnp.concatenate([sin, cos], axis=1)
    inner = jnp.stack(
        [real.reshape(high, LOW, 2 * modes), imag.reshape(high, LOW, 2 * modes)], axis=1
    ).reshape(2 * PHI_T, 2 * modes)
    zero = jnp.zeros((1, 2 * modes), jnp.float32)
    edge = jnp.concatenate([real[LOW::LOW], zero, imag[LOW::LOW], zero], axis=0)
    return jnp.concatenate([inner, edge], axis=0).astype(jnp.bfloat16)


def psi_rows(orders):
    order = jnp.arange(orders, dtype=jnp.int32)[:, None]
    cos, sin = wave_table(NPSI, jnp.arange(NPSI, dtype=jnp.int32)[None, :], order)
    half = jnp.concatenate([cos, -sin], axis=0).astype(jnp.bfloat16)
    return jnp.concatenate([half, half], axis=1)


def shards(sky_coeffs, beam_coeffs, wigner, visits, point_slot, phi_cell, psi_cell, fraction):
    order_count = lax.axis_size("order")
    shard_count = lax.axis_size("shard")
    local_modes = sky_coeffs.shape[0]
    local_orders = beam_coeffs.shape[0]
    theta_count = wigner.shape[3]
    orders = local_orders * order_count
    modes = local_modes * shard_count
    weighted = (sky_coeffs[:, None, :, :] * beam_coeffs[None, :, None, :]).astype(jnp.bfloat16)
    coeffs = jnp.einsum("mkcl,mklt->mkct", weighted, wigner, preferred_element_type=jnp.float32)
    coeffs = coeffs.astype(jnp.bfloat16).reshape(local_modes * local_orders * 2, theta_count)
    coeffs = lax.all_gather(coeffs, "shard", axis=0, tiled=True)
    if order_count > 1:
        coeffs = coeffs.reshape(modes, local_orders * 2, theta_count)
        coeffs = lax.all_gather(coeffs, "order", axis=1, tiled=True)
        coeffs = coeffs.reshape(modes * orders * 2, theta_count)

    blocks = NPHI // (order_count * PHI_T)
    owners, depth = visits.shape[1], visits.shape[2]
    slots = owners * depth
    tile = jnp.maximum(visits[0], 0).reshape(1, slots)
    owner = (jnp.arange(slots, dtype=jnp.int32) // depth)[None, :]
    row = (owner % shard_count) * (theta_count // shard_count) + tile // blocks
    first_phi = (owner // shard_count) * (NPHI // order_count) + (tile % blocks) * PHI_T
    turn_cos, turn_sin = wave_table(
        NPHI, first_phi, jnp.arange(modes, dtype=jnp.int32)[:, None]
    )
    count = point_slot.shape[0]
    chunks = count // CHUNK
    lined = (chunks, 1, CHUNK)
    pairs = jnp.transpose(fraction.reshape(2, chunks, CHUNK), (1, 0, 2))
    high = PHI_T // LOW
    timeline = pl.pallas_call(
        functools.partial(interpolate, modes, orders),
        out_shape=jax.ShapeDtypeStruct(lined, jnp.float32),
        in_specs=[pl.BlockSpec(memory_space=pltpu.VMEM)] * 10,
        out_specs=pl.BlockSpec(memory_space=pltpu.VMEM),
        scratch_shapes=[
            pltpu.VMEM((modes * orders * 2, LANES), jnp.float32),
            pltpu.VMEM((orders * 2 * high, LANES), jnp.float32),
            pltpu.VMEM((orders * 2 * (LOW + 1), high * slots), jnp.bfloat16),
            pltpu.VMEM((orders * 2, CHUNK), jnp.float32),
        ],
    )(
        coeffs,
        row,
        turn_cos,
        turn_sin,
        phi_rows(modes),
        psi_rows(orders),
        point_slot.reshape(lined),
        phi_cell.reshape(lined),
        psi_cell.reshape(lined),
        pairs,
    )
    return timeline.reshape(count)


def solution(mesh):
    placed = (
        P("shard", None, None),
        P("order", None),
        P("shard", "order", None, None),
        P(("order", "shard"), None, None),
        P(("order", "shard")),
        P(("order", "shard")),
        P(("order", "shard")),
        P(None, ("order", "shard")),
    )
    return jax.shard_map(
        shards, mesh=mesh, in_specs=placed, out_specs=P(("order", "shard")), check_vma=False
    )
```

```python
import functools
import math

import jax
import jax.numpy as jnp
import numpy as np
from jax import lax
from jax.experimental import pallas as pl
from jax.experimental.pallas import tpu as pltpu
from jax.sharding import PartitionSpec as P

NPHI = 4096
NPSI = 128
PHI_T = 32
LOW = 8
LANES = 128
CHUNK = 256


SQUARE = 4
CORES = 2


def gather_blocks(lines, block_ref, out_ref, send_sem, recv_sem):
    me = lax.axis_index("shard")
    core = me % CORES
    square = me // CORES % SQUARE
    line = me // (CORES * SQUARE)
    depth = block_ref.shape[0]

    def index(at_line, at_square, at_core):
        return (at_line * SQUARE + at_square) * CORES + at_core

    along = [(line + d) % lines for d in range(1, lines)]
    across = [(square + d) % SQUARE for d in range(1, SQUARE)]
    other = (core + 1) % CORES
    line_peers = [index(a, square, core) for a in along]
    square_peers = [index(line, b, core) for b in across]
    twin = index(line, square, other)
    barrier = pltpu.get_barrier_semaphore()
    peers = line_peers + square_peers + [twin]
    for peer in peers:
        pl.semaphore_signal(
            barrier, inc=1, device_id={"shard": peer}, device_id_type=pl.DeviceIdType.MESH
        )
    pl.semaphore_wait(barrier, len(peers))

    started = []

    def place(owner):
        return out_ref.at[pl.ds(pl.multiple_of(owner * depth, depth), depth), :]

    def send(source, owner, peer):
        copy = pltpu.make_async_remote_copy(
            src_ref=source,
            dst_ref=place(owner),
            send_sem=send_sem.at[len(started)],
            recv_sem=recv_sem.at[owner],
            device_id={"shard": peer},
            device_id_type=pl.DeviceIdType.MESH,
        )
        copy.start()
        started.append(copy)

    def arrive(owner):
        pltpu.make_async_remote_copy(
            src_ref=place(owner),
            dst_ref=place(owner),
            send_sem=send_sem.at[0],
            recv_sem=recv_sem.at[owner],
            device_id={"shard": twin},
            device_id_type=pl.DeviceIdType.MESH,
        ).wait_recv()

    for peer in line_peers + square_peers + [twin]:
        send(block_ref, me, peer)
    out_ref[pl.ds(pl.multiple_of(me * depth, depth), depth), :] = block_ref[...]
    for owner in line_peers:
        arrive(owner)
        for peer in square_peers + [twin]:
            send(place(owner), owner, peer)
    for a in [line] + along:
        for b in across:
            owner = index(a, b, core)
            arrive(owner)
            send(place(owner), owner, twin)
    for a in [line] + along:
        for b in [square] + across:
            arrive(index(a, b, other))
    for copy in started:
        copy.wait_send()


def wave_table(count, grid, mode):
    phase = 2.0 * math.pi * ((grid * mode) % count) / count
    return np.cos(phase), np.sin(phase)


def interpolate(
    modes,
    orders,
    order_count,
    shard_count,
    depth,
    coeffs_ref,
    visit_ref,
    phi_table_ref,
    psi_table_ref,
    slot_ref,
    phi_ref,
    psi_ref,
    fraction_ref,
    out_ref,
    picked,
    edge,
    synth,
    wave,
):
    terms = 2 * orders
    high = PHI_T // LOW
    theta, slots = coeffs_ref.shape[1], visit_ref.shape[1]
    blocks = NPHI // (order_count * PHI_T)
    groups = slots // LANES
    for g in range(groups):
        lanes = slice(g * LANES, (g + 1) * LANES)
        tile = jnp.maximum(visit_ref[:, lanes], 0)
        owner = (lax.broadcasted_iota(jnp.int32, (1, LANES), 1) + g * LANES) // depth
        row = (owner % shard_count) * (theta // shard_count) + tile // blocks
        first_phi = (owner // shard_count) * (NPHI // order_count) + (tile % blocks) * PHI_T
        chosen = (
            lax.broadcasted_iota(jnp.int32, (theta, LANES), 0) == row
        ).astype(jnp.float32).astype(jnp.bfloat16)

        def pick(m, carry):
            rows = pl.ds(pl.multiple_of(m * 4 * terms, 4 * terms), 4 * terms)
            picked[rows, :] = jnp.dot(
                coeffs_ref[rows, :], chosen, preferred_element_type=jnp.float32
            )
            return carry

        lax.fori_loop(0, modes // 4, pick, 0)
        turn = (lax.broadcasted_iota(jnp.int32, (modes, LANES), 0) * first_phi) % NPHI
        angle = turn.astype(jnp.float32) * (2.0 * math.pi / NPHI)
        turn_cos, turn_sin = jnp.cos(angle), jnp.sin(angle)

        def sum_modes(k, carry):
            real = picked[pl.ds(2 * k, modes, stride=terms), :]
            imag = picked[pl.ds(2 * k + 1, modes, stride=terms), :]
            turned = jnp.concatenate(
                [turn_cos * real - turn_sin * imag, turn_sin * real + turn_cos * imag], axis=0
            ).astype(jnp.bfloat16)
            values = jnp.dot(phi_table_ref[...], turned, preferred_element_type=jnp.float32)
            for h in range(high):
                synth[
                    pl.ds(pl.multiple_of(k * 2 * LOW, 2 * LOW), 2 * LOW),
                    h * slots + g * LANES : h * slots + (g + 1) * LANES,
                ] = values[h * 2 * LOW : (h + 1) * 2 * LOW].astype(jnp.bfloat16)
            edge[pl.ds(pl.multiple_of(k * 2 * high, 2 * high), 2 * high), :] = values[
                2 * PHI_T :
            ]
            return carry

        lax.fori_loop(0, orders, sum_modes, 0, unroll=4)
        for part in range(2):
            for h in range(high):
                synth[
                    terms * LOW + part * orders : terms * LOW + (part + 1) * orders,
                    h * slots + g * LANES : h * slots + (g + 1) * LANES,
                ] = edge[pl.ds(part * high + h, orders, stride=2 * high), :].astype(jnp.bfloat16)

    def chunk(i, carry):
        phi, psi = phi_ref[i], psi_ref[i]
        along = fraction_ref[i]
        along_phi, along_psi = along[0:1], along[1:2]
        key = (phi // LOW) * slots + slot_ref[i]
        entry = (
            lax.broadcasted_iota(jnp.int32, (high * slots, CHUNK), 0) == key
        ).astype(jnp.float32).astype(jnp.bfloat16)
        at_psi = lax.broadcasted_iota(jnp.int32, (NPSI, CHUNK), 0)
        weight = jnp.where(
            at_psi == psi, 1.0 - along_psi, jnp.where(at_psi == (psi + 1) % NPSI, along_psi, 0.0)
        )
        coarse = weight.astype(jnp.bfloat16)
        fine = (weight - coarse.astype(jnp.float32)).astype(jnp.bfloat16)
        waves = jnp.dot(
            psi_table_ref[...],
            jnp.concatenate([coarse, fine], axis=0),
            preferred_element_type=jnp.float32,
        )
        wave[...] = waves
        values = jnp.dot(synth[...], entry, preferred_element_type=jnp.float32)
        sums = [jnp.zeros((LOW, CHUNK), jnp.float32) for _ in range(4)]
        for k in range(orders):
            for part in range(2):
                at = (2 * k + part) * LOW
                line = part * orders + k
                sums[at // LOW % 4] += values[at : at + LOW] * wave[line : line + 1, :]
        inner = (sums[0] + sums[1]) + (sums[2] + sums[3])
        last = jnp.sum(values[terms * LOW :] * waves, axis=0, keepdims=True)
        low = phi % LOW
        at_low = lax.broadcasted_iota(jnp.int32, (LOW, CHUNK), 0)
        weight_phi = jnp.where(
            at_low == low, 1.0 - along_phi, jnp.where(at_low == low + 1, along_phi, 0.0)
        )
        total = jnp.sum(inner * weight_phi, axis=0, keepdims=True)
        out_ref[i] = total + jnp.where(low == LOW - 1, along_phi, 0.0) * last
        return carry

    lax.fori_loop(0, slot_ref.shape[0], chunk, 0)


def phi_rows(modes):
    mode = np.arange(modes, dtype=np.int64)[None, :]
    high = PHI_T // LOW
    cos, sin = wave_table(NPHI, np.arange(PHI_T, dtype=np.int64)[:, None], mode)
    real = np.concatenate([cos, -sin], axis=1)
    imag = np.concatenate([sin, cos], axis=1)
    inner = np.stack(
        [real.reshape(high, LOW, 2 * modes), imag.reshape(high, LOW, 2 * modes)], axis=1
    ).reshape(2 * PHI_T, 2 * modes)
    zero = np.zeros((1, 2 * modes), np.float64)
    edge = np.concatenate([real[LOW::LOW], zero, imag[LOW::LOW], zero], axis=0)
    return jnp.asarray(np.concatenate([inner, edge], axis=0), jnp.bfloat16)


def psi_rows(orders):
    order = np.arange(orders, dtype=np.int64)[:, None]
    cos, sin = wave_table(NPSI, np.arange(NPSI, dtype=np.int64)[None, :], order)
    half = np.concatenate([cos, -sin], axis=0)
    return jnp.asarray(np.concatenate([half, half], axis=1), jnp.bfloat16)


def shards(sky_coeffs, beam_coeffs, wigner, visits, point_slot, phi_cell, psi_cell, fraction):
    order_count = lax.axis_size("order")
    shard_count = lax.axis_size("shard")
    local_modes = sky_coeffs.shape[0]
    local_orders = beam_coeffs.shape[0]
    theta_count = wigner.shape[3]
    orders = local_orders * order_count
    modes = local_modes * shard_count
    weighted = (sky_coeffs[:, None, :, :] * beam_coeffs[None, :, None, :]).astype(jnp.bfloat16)
    coeffs = jnp.einsum("mkcl,mklt->mkct", weighted, wigner, preferred_element_type=jnp.float32)
    coeffs = coeffs.astype(jnp.bfloat16).reshape(local_modes * local_orders * 2, theta_count)
    coeffs = pl.pallas_call(
        functools.partial(gather_blocks, shard_count // (SQUARE * CORES)),
        out_shape=jax.ShapeDtypeStruct((shard_count * coeffs.shape[0], theta_count), jnp.bfloat16),
        in_specs=[pl.BlockSpec(memory_space=pltpu.VMEM)],
        out_specs=pl.BlockSpec(memory_space=pltpu.VMEM),
        scratch_shapes=[
            pltpu.SemaphoreType.DMA((shard_count - 1,)),
            pltpu.SemaphoreType.DMA((shard_count,)),
        ],
        compiler_params=pltpu.CompilerParams(collective_id=0, has_side_effects=True),
    )(coeffs)
    if order_count > 1:
        coeffs = coeffs.reshape(modes, local_orders * 2, theta_count)
        coeffs = lax.all_gather(coeffs, "order", axis=1, tiled=True)
        coeffs = coeffs.reshape(modes * orders * 2, theta_count)

    slots = visits.shape[1] * visits.shape[2]
    count = point_slot.shape[0]
    chunks = count // CHUNK
    lined = (chunks, 1, CHUNK)
    pairs = jnp.transpose(fraction.reshape(2, chunks, CHUNK), (1, 0, 2))
    high = PHI_T // LOW
    timeline = pl.pallas_call(
        functools.partial(
            interpolate, modes, orders, order_count, shard_count, visits.shape[2]
        ),
        out_shape=jax.ShapeDtypeStruct(lined, jnp.float32),
        in_specs=[pl.BlockSpec(memory_space=pltpu.VMEM)] * 8,
        out_specs=pl.BlockSpec(memory_space=pltpu.VMEM),
        scratch_shapes=[
            pltpu.VMEM((modes * orders * 2, LANES), jnp.float32),
            pltpu.VMEM((orders * 2 * high, LANES), jnp.float32),
            pltpu.VMEM((orders * 2 * (LOW + 1), high * slots), jnp.bfloat16),
            pltpu.VMEM((orders * 2, CHUNK), jnp.float32),
        ],
    )(
        coeffs,
        visits.reshape(1, slots),
        phi_rows(modes),
        psi_rows(orders),
        point_slot.reshape(lined),
        phi_cell.reshape(lined),
        psi_cell.reshape(lined),
        pairs,
    )
    return timeline.reshape(count)


def solution(mesh):
    placed = (
        P("shard", None, None),
        P("order", None),
        P("shard", "order", None, None),
        P(("order", "shard"), None, None),
        P(("order", "shard")),
        P(("order", "shard")),
        P(("order", "shard")),
        P(None, ("order", "shard")),
    )
    return jax.shard_map(
        shards, mesh=mesh, in_specs=placed, out_specs=P(("order", "shard")), check_vma=False
    )
```

```python
import functools
import math

import jax
import jax.numpy as jnp
import numpy as np
from jax import lax
from jax.experimental import pallas as pl
from jax.experimental.pallas import tpu as pltpu
from jax.sharding import PartitionSpec as P

NPHI = 4096
NPSI = 128
PHI_T = 32
LOW = 8
LANES = 128
CHUNK = 256


SQUARE = 4
CORES = 2


def gather_blocks(lines, block_ref, out_ref, send_sem, recv_sem):
    me = lax.axis_index("shard")
    core = me % CORES
    square = me // CORES % SQUARE
    line = me // (CORES * SQUARE)
    depth = block_ref.shape[0]

    def index(at_line, at_square, at_core):
        return (at_line * SQUARE + at_square) * CORES + at_core

    along = [(line + d) % lines for d in range(1, lines)]
    across = [(square + d) % SQUARE for d in range(1, SQUARE)]
    other = (core + 1) % CORES
    line_peers = [index(a, square, core) for a in along]
    square_peers = [index(line, b, core) for b in across]
    twin = index(line, square, other)
    barrier = pltpu.get_barrier_semaphore()
    peers = line_peers + square_peers + [twin]
    for peer in peers:
        pl.semaphore_signal(
            barrier, inc=1, device_id={"shard": peer}, device_id_type=pl.DeviceIdType.MESH
        )
    pl.semaphore_wait(barrier, len(peers))

    started = []

    def place(owner):
        return out_ref.at[pl.ds(pl.multiple_of(owner * depth, depth), depth), :]

    def send(source, owner, peer):
        copy = pltpu.make_async_remote_copy(
            src_ref=source,
            dst_ref=place(owner),
            send_sem=send_sem.at[len(started)],
            recv_sem=recv_sem.at[owner],
            device_id={"shard": peer},
            device_id_type=pl.DeviceIdType.MESH,
        )
        copy.start()
        started.append(copy)

    def arrive(owner):
        pltpu.make_async_remote_copy(
            src_ref=place(owner),
            dst_ref=place(owner),
            send_sem=send_sem.at[0],
            recv_sem=recv_sem.at[owner],
            device_id={"shard": twin},
            device_id_type=pl.DeviceIdType.MESH,
        ).wait_recv()

    for peer in line_peers + square_peers + [twin]:
        send(block_ref, me, peer)
    out_ref[pl.ds(pl.multiple_of(me * depth, depth), depth), :] = block_ref[...]
    for owner in line_peers:
        arrive(owner)
        for peer in square_peers + [twin]:
            send(place(owner), owner, peer)
    for a in [line] + along:
        for b in across:
            owner = index(a, b, core)
            arrive(owner)
            send(place(owner), owner, twin)
    for a in [line] + along:
        for b in [square] + across:
            arrive(index(a, b, other))
    for copy in started:
        copy.wait_send()


def wave_table(count, grid, mode):
    phase = 2.0 * math.pi * ((grid * mode) % count) / count
    return np.cos(phase), np.sin(phase)


def interpolate(
    modes,
    orders,
    order_count,
    shard_count,
    depth,
    coeffs_ref,
    visit_ref,
    phi_table_ref,
    psi_table_ref,
    slot_ref,
    phi_ref,
    psi_ref,
    fraction_ref,
    out_ref,
    picked,
    edge,
    synth,
    wave_a,
    wave_b,
    values_a,
    values_b,
):
    terms = 2 * orders
    high = PHI_T // LOW
    theta, slots = coeffs_ref.shape[1], visit_ref.shape[1]
    blocks = NPHI // (order_count * PHI_T)
    groups = slots // LANES
    for g in range(groups):
        lanes = slice(g * LANES, (g + 1) * LANES)
        tile = jnp.maximum(visit_ref[:, lanes], 0)
        owner = (lax.broadcasted_iota(jnp.int32, (1, LANES), 1) + g * LANES) // depth
        row = (owner % shard_count) * (theta // shard_count) + tile // blocks
        first_phi = (owner // shard_count) * (NPHI // order_count) + (tile % blocks) * PHI_T
        chosen = (
            lax.broadcasted_iota(jnp.int32, (theta, LANES), 0) == row
        ).astype(jnp.float32).astype(jnp.bfloat16)

        def pick(m, carry):
            rows = pl.ds(pl.multiple_of(m * 4 * terms, 4 * terms), 4 * terms)
            picked[rows, :] = jnp.dot(
                coeffs_ref[rows, :], chosen, preferred_element_type=jnp.float32
            )
            return carry

        lax.fori_loop(0, modes // 4, pick, 0)
        turn = (lax.broadcasted_iota(jnp.int32, (modes, LANES), 0) * first_phi) % NPHI
        angle = turn.astype(jnp.float32) * (2.0 * math.pi / NPHI)
        turn_cos, turn_sin = jnp.cos(angle), jnp.sin(angle)

        def sum_modes(k, carry):
            real = picked[pl.ds(2 * k, modes, stride=terms), :]
            imag = picked[pl.ds(2 * k + 1, modes, stride=terms), :]
            turned = jnp.concatenate(
                [turn_cos * real - turn_sin * imag, turn_sin * real + turn_cos * imag], axis=0
            ).astype(jnp.bfloat16)
            values = jnp.dot(phi_table_ref[...], turned, preferred_element_type=jnp.float32)
            for h in range(high):
                synth[
                    pl.ds(pl.multiple_of(k * 2 * LOW, 2 * LOW), 2 * LOW),
                    h * slots + g * LANES : h * slots + (g + 1) * LANES,
                ] = values[h * 2 * LOW : (h + 1) * 2 * LOW].astype(jnp.bfloat16)
            edge[pl.ds(pl.multiple_of(k * 2 * high, 2 * high), 2 * high), :] = values[
                2 * PHI_T :
            ]
            return carry

        lax.fori_loop(0, orders, sum_modes, 0, unroll=4)
        for part in range(2):
            for h in range(high):
                synth[
                    terms * LOW + part * orders : terms * LOW + (part + 1) * orders,
                    h * slots + g * LANES : h * slots + (g + 1) * LANES,
                ] = edge[pl.ds(part * high + h, orders, stride=2 * high), :].astype(jnp.bfloat16)

    def begin(i, values, wave):
        phi, psi = phi_ref[i], psi_ref[i]
        along_psi = fraction_ref[i][1:2]
        key = (phi // LOW) * slots + slot_ref[i]
        entry = (
            lax.broadcasted_iota(jnp.int32, (high * slots, CHUNK), 0) == key
        ).astype(jnp.float32).astype(jnp.bfloat16)
        at_psi = lax.broadcasted_iota(jnp.int32, (NPSI, CHUNK), 0)
        weight = jnp.where(
            at_psi == psi, 1.0 - along_psi, jnp.where(at_psi == (psi + 1) % NPSI, along_psi, 0.0)
        )
        coarse = weight.astype(jnp.bfloat16)
        fine = (weight - coarse.astype(jnp.float32)).astype(jnp.bfloat16)
        wave[...] = jnp.dot(
            psi_table_ref[...],
            jnp.concatenate([coarse, fine], axis=0),
            preferred_element_type=jnp.float32,
        )
        values[...] = jnp.dot(synth[...], entry, preferred_element_type=jnp.float32)

    def finish(i, values, wave):
        phi = phi_ref[i]
        along_phi = fraction_ref[i][0:1]
        sums = [jnp.zeros((LOW, CHUNK), jnp.float32) for _ in range(4)]
        for k in range(orders):
            for part in range(2):
                at = (2 * k + part) * LOW
                line = part * orders + k
                sums[at // LOW % 4] += values[at : at + LOW, :] * wave[line : line + 1, :]
        inner = (sums[0] + sums[1]) + (sums[2] + sums[3])
        last = jnp.sum(values[terms * LOW :, :] * wave[...], axis=0, keepdims=True)
        low = phi % LOW
        at_low = lax.broadcasted_iota(jnp.int32, (LOW, CHUNK), 0)
        weight_phi = jnp.where(
            at_low == low, 1.0 - along_phi, jnp.where(at_low == low + 1, along_phi, 0.0)
        )
        total = jnp.sum(inner * weight_phi, axis=0, keepdims=True)
        out_ref[i] = total + jnp.where(low == LOW - 1, along_phi, 0.0) * last

    chunks = slot_ref.shape[0]
    begin(0, values_a, wave_a)

    def pair(i, carry):
        begin(2 * i + 1, values_b, wave_b)
        finish(2 * i, values_a, wave_a)
        begin(jnp.minimum(2 * i + 2, chunks - 1), values_a, wave_a)
        finish(2 * i + 1, values_b, wave_b)
        return carry

    lax.fori_loop(0, chunks // 2, pair, 0)


def phi_rows(modes):
    mode = np.arange(modes, dtype=np.int64)[None, :]
    high = PHI_T // LOW
    cos, sin = wave_table(NPHI, np.arange(PHI_T, dtype=np.int64)[:, None], mode)
    real = np.concatenate([cos, -sin], axis=1)
    imag = np.concatenate([sin, cos], axis=1)
    inner = np.stack(
        [real.reshape(high, LOW, 2 * modes), imag.reshape(high, LOW, 2 * modes)], axis=1
    ).reshape(2 * PHI_T, 2 * modes)
    zero = np.zeros((1, 2 * modes), np.float64)
    edge = np.concatenate([real[LOW::LOW], zero, imag[LOW::LOW], zero], axis=0)
    return jnp.asarray(np.concatenate([inner, edge], axis=0), jnp.bfloat16)


def psi_rows(orders):
    order = np.arange(orders, dtype=np.int64)[:, None]
    cos, sin = wave_table(NPSI, np.arange(NPSI, dtype=np.int64)[None, :], order)
    half = np.concatenate([cos, -sin], axis=0)
    return jnp.asarray(np.concatenate([half, half], axis=1), jnp.bfloat16)


def shards(sky_coeffs, beam_coeffs, wigner, visits, point_slot, phi_cell, psi_cell, fraction):
    order_count = lax.axis_size("order")
    shard_count = lax.axis_size("shard")
    local_modes = sky_coeffs.shape[0]
    local_orders = beam_coeffs.shape[0]
    theta_count = wigner.shape[3]
    orders = local_orders * order_count
    modes = local_modes * shard_count
    weighted = (sky_coeffs[:, None, :, :] * beam_coeffs[None, :, None, :]).astype(jnp.bfloat16)
    coeffs = jnp.einsum("mkcl,mklt->mkct", weighted, wigner, preferred_element_type=jnp.float32)
    coeffs = coeffs.astype(jnp.bfloat16).reshape(local_modes * local_orders * 2, theta_count)
    coeffs = pl.pallas_call(
        functools.partial(gather_blocks, shard_count // (SQUARE * CORES)),
        out_shape=jax.ShapeDtypeStruct((shard_count * coeffs.shape[0], theta_count), jnp.bfloat16),
        in_specs=[pl.BlockSpec(memory_space=pltpu.VMEM)],
        out_specs=pl.BlockSpec(memory_space=pltpu.VMEM),
        scratch_shapes=[
            pltpu.SemaphoreType.DMA((shard_count - 1,)),
            pltpu.SemaphoreType.DMA((shard_count,)),
        ],
        compiler_params=pltpu.CompilerParams(collective_id=0, has_side_effects=True),
    )(coeffs)
    if order_count > 1:
        coeffs = coeffs.reshape(modes, local_orders * 2, theta_count)
        coeffs = lax.all_gather(coeffs, "order", axis=1, tiled=True)
        coeffs = coeffs.reshape(modes * orders * 2, theta_count)

    slots = visits.shape[1] * visits.shape[2]
    count = point_slot.shape[0]
    chunks = count // CHUNK
    lined = (chunks, 1, CHUNK)
    pairs = jnp.transpose(fraction.reshape(2, chunks, CHUNK), (1, 0, 2))
    high = PHI_T // LOW
    timeline = pl.pallas_call(
        functools.partial(
            interpolate, modes, orders, order_count, shard_count, visits.shape[2]
        ),
        out_shape=jax.ShapeDtypeStruct(lined, jnp.float32),
        in_specs=[pl.BlockSpec(memory_space=pltpu.VMEM)] * 8,
        out_specs=pl.BlockSpec(memory_space=pltpu.VMEM),
        scratch_shapes=[
            pltpu.VMEM((modes * orders * 2, LANES), jnp.float32),
            pltpu.VMEM((orders * 2 * high, LANES), jnp.float32),
            pltpu.VMEM((orders * 2 * (LOW + 1), high * slots), jnp.bfloat16),
            pltpu.VMEM((orders * 2, CHUNK), jnp.float32),
            pltpu.VMEM((orders * 2, CHUNK), jnp.float32),
            pltpu.VMEM((orders * 2 * (LOW + 1), CHUNK), jnp.float32),
            pltpu.VMEM((orders * 2 * (LOW + 1), CHUNK), jnp.float32),
        ],
    )(
        coeffs,
        visits.reshape(1, slots),
        phi_rows(modes),
        psi_rows(orders),
        point_slot.reshape(lined),
        phi_cell.reshape(lined),
        psi_cell.reshape(lined),
        pairs,
    )
    return timeline.reshape(count)


def solution(mesh):
    placed = (
        P("shard", None, None),
        P("order", None),
        P("shard", "order", None, None),
        P(("order", "shard"), None, None),
        P(("order", "shard")),
        P(("order", "shard")),
        P(("order", "shard")),
        P(None, ("order", "shard")),
    )
    return jax.shard_map(
        shards, mesh=mesh, in_specs=placed, out_specs=P(("order", "shard")), check_vma=False
    )
```

```python
import functools
import math

import jax
import jax.numpy as jnp
import numpy as np
from jax import lax
from jax.experimental import pallas as pl
from jax.experimental.pallas import tpu as pltpu
from jax.sharding import PartitionSpec as P

NPHI = 4096
NPSI = 128
PHI_T = 32
LOW = 8
LANES = 128
CHUNK = 256


SQUARE = 4
CORES = 2


def gather_blocks(lines, block_ref, out_ref, send_sem, recv_sem):
    me = lax.axis_index("shard")
    core = me % CORES
    square = me // CORES % SQUARE
    line = me // (CORES * SQUARE)
    depth = block_ref.shape[0]

    def index(at_line, at_square, at_core):
        return (at_line * SQUARE + at_square) * CORES + at_core

    along = [(line + d) % lines for d in range(1, lines)]
    if lines == 4:
        half = line // 2
        along = [line + 1 - 2 * (line % 2), 2 - half, 3 - 3 * half]
    across = [(square + d) % SQUARE for d in range(1, SQUARE)]
    other = (core + 1) % CORES
    line_peers = [index(a, square, core) for a in along]
    square_peers = [index(line, b, core) for b in across]
    twin = index(line, square, other)
    barrier = pltpu.get_barrier_semaphore()
    peers = line_peers + square_peers + [twin]
    for peer in peers:
        pl.semaphore_signal(
            barrier, inc=1, device_id={"shard": peer}, device_id_type=pl.DeviceIdType.MESH
        )
    pl.semaphore_wait(barrier, len(peers))

    started = []

    def place(owner):
        return out_ref.at[pl.ds(pl.multiple_of(owner * depth, depth), depth), :]

    def send(source, owner, peer):
        copy = pltpu.make_async_remote_copy(
            src_ref=source,
            dst_ref=place(owner),
            send_sem=send_sem.at[len(started)],
            recv_sem=recv_sem.at[owner],
            device_id={"shard": peer},
            device_id_type=pl.DeviceIdType.MESH,
        )
        copy.start()
        started.append(copy)

    def arrive(owner):
        pltpu.make_async_remote_copy(
            src_ref=place(owner),
            dst_ref=place(owner),
            send_sem=send_sem.at[0],
            recv_sem=recv_sem.at[owner],
            device_id={"shard": twin},
            device_id_type=pl.DeviceIdType.MESH,
        ).wait_recv()

    for peer in line_peers[::-1] + square_peers + [twin]:
        send(block_ref, me, peer)
    out_ref[pl.ds(pl.multiple_of(me * depth, depth), depth), :] = block_ref[...]
    for owner in line_peers:
        arrive(owner)
        for peer in square_peers + [twin]:
            send(place(owner), owner, peer)
    for a in [line] + along:
        for b in across:
            owner = index(a, b, core)
            arrive(owner)
            send(place(owner), owner, twin)
    for a in [line] + along:
        for b in [square] + across:
            arrive(index(a, b, other))
    for copy in started:
        copy.wait_send()


def wave_table(count, grid, mode):
    phase = 2.0 * math.pi * ((grid * mode) % count) / count
    return np.cos(phase), np.sin(phase)


def interpolate(
    modes,
    orders,
    order_count,
    shard_count,
    coeffs_ref,
    visit_ref,
    phi_table_ref,
    psi_table_ref,
    slot_ref,
    phi_ref,
    psi_ref,
    fraction_ref,
    out_ref,
    picked,
    edge,
    synth,
    wave_a,
    wave_b,
    values_a,
    values_b,
):
    terms = 2 * orders
    high = PHI_T // LOW
    theta = coeffs_ref.shape[1]
    depth, owners = visit_ref.shape
    slots = owners * depth
    blocks = NPHI // (order_count * PHI_T)
    groups = slots // LANES
    listed = jnp.concatenate([visit_ref[d : d + 1, :] for d in range(depth)], axis=1)
    for g in range(groups):
        lanes = slice(g * LANES, (g + 1) * LANES)
        tile = jnp.maximum(listed[:, lanes], 0)
        owner = (lax.broadcasted_iota(jnp.int32, (1, LANES), 1) + g * LANES) % owners
        row = (owner % shard_count) * (theta // shard_count) + tile // blocks
        first_phi = (owner // shard_count) * (NPHI // order_count) + (tile % blocks) * PHI_T
        chosen = (
            lax.broadcasted_iota(jnp.int32, (theta, LANES), 0) == row
        ).astype(jnp.float32).astype(jnp.bfloat16)

        def pick(m, carry):
            rows = pl.ds(pl.multiple_of(m * 4 * terms, 4 * terms), 4 * terms)
            picked[rows, :] = jnp.dot(
                coeffs_ref[rows, :], chosen, preferred_element_type=jnp.float32
            )
            return carry

        lax.fori_loop(0, modes // 4, pick, 0)
        turn = (lax.broadcasted_iota(jnp.int32, (modes, LANES), 0) * first_phi) % NPHI
        angle = turn.astype(jnp.float32) * (2.0 * math.pi / NPHI)
        turn_cos, turn_sin = jnp.cos(angle), jnp.sin(angle)

        def sum_modes(k, carry):
            real = picked[pl.ds(2 * k, modes, stride=terms), :]
            imag = picked[pl.ds(2 * k + 1, modes, stride=terms), :]
            turned = jnp.concatenate(
                [turn_cos * real - turn_sin * imag, turn_sin * real + turn_cos * imag], axis=0
            ).astype(jnp.bfloat16)
            values = jnp.dot(phi_table_ref[...], turned, preferred_element_type=jnp.float32)
            for h in range(high):
                synth[
                    pl.ds(pl.multiple_of(k * 2 * LOW, 2 * LOW), 2 * LOW),
                    h * slots + g * LANES : h * slots + (g + 1) * LANES,
                ] = values[h * 2 * LOW : (h + 1) * 2 * LOW].astype(jnp.bfloat16)
            edge[pl.ds(pl.multiple_of(k * 2 * high, 2 * high), 2 * high), :] = values[
                2 * PHI_T :
            ]
            return carry

        lax.fori_loop(0, orders, sum_modes, 0, unroll=4)
        for part in range(2):
            for h in range(high):
                synth[
                    terms * LOW + part * orders : terms * LOW + (part + 1) * orders,
                    h * slots + g * LANES : h * slots + (g + 1) * LANES,
                ] = edge[pl.ds(part * high + h, orders, stride=2 * high), :].astype(jnp.bfloat16)

    def begin(i, values, wave):
        phi, psi = phi_ref[i], psi_ref[i]
        along_psi = fraction_ref[i][1:2]
        slot = slot_ref[i]
        key = ((phi // LOW) * depth + slot % depth) * owners + slot // depth
        entry = (
            lax.broadcasted_iota(jnp.int32, (high * slots, CHUNK), 0) == key
        ).astype(jnp.float32).astype(jnp.bfloat16)
        at_psi = lax.broadcasted_iota(jnp.int32, (NPSI, CHUNK), 0)
        weight = jnp.where(
            at_psi == psi, 1.0 - along_psi, jnp.where(at_psi == (psi + 1) % NPSI, along_psi, 0.0)
        )
        coarse = weight.astype(jnp.bfloat16)
        fine = (weight - coarse.astype(jnp.float32)).astype(jnp.bfloat16)
        wave[...] = jnp.dot(
            psi_table_ref[...],
            jnp.concatenate([coarse, fine], axis=0),
            preferred_element_type=jnp.float32,
        )
        values[...] = jnp.dot(synth[...], entry, preferred_element_type=jnp.float32)

    def finish(i, values, wave):
        phi = phi_ref[i]
        along_phi = fraction_ref[i][0:1]
        sums = [jnp.zeros((LOW, CHUNK), jnp.float32) for _ in range(4)]
        for k in range(orders):
            for part in range(2):
                at = (2 * k + part) * LOW
                line = part * orders + k
                sums[at // LOW % 4] += values[at : at + LOW, :] * wave[line : line + 1, :]
        inner = (sums[0] + sums[1]) + (sums[2] + sums[3])
        last = jnp.sum(values[terms * LOW :, :] * wave[...], axis=0, keepdims=True)
        low = phi % LOW
        at_low = lax.broadcasted_iota(jnp.int32, (LOW, CHUNK), 0)
        weight_phi = jnp.where(
            at_low == low, 1.0 - along_phi, jnp.where(at_low == low + 1, along_phi, 0.0)
        )
        total = jnp.sum(inner * weight_phi, axis=0, keepdims=True)
        out_ref[i] = total + jnp.where(low == LOW - 1, along_phi, 0.0) * last

    chunks = slot_ref.shape[0]
    begin(0, values_a, wave_a)

    def pair(i, carry):
        begin(2 * i + 1, values_b, wave_b)
        finish(2 * i, values_a, wave_a)
        begin(jnp.minimum(2 * i + 2, chunks - 1), values_a, wave_a)
        finish(2 * i + 1, values_b, wave_b)
        return carry

    lax.fori_loop(0, chunks // 2, pair, 0)


def phi_rows(modes):
    mode = np.arange(modes, dtype=np.int64)[None, :]
    high = PHI_T // LOW
    cos, sin = wave_table(NPHI, np.arange(PHI_T, dtype=np.int64)[:, None], mode)
    real = np.concatenate([cos, -sin], axis=1)
    imag = np.concatenate([sin, cos], axis=1)
    inner = np.stack(
        [real.reshape(high, LOW, 2 * modes), imag.reshape(high, LOW, 2 * modes)], axis=1
    ).reshape(2 * PHI_T, 2 * modes)
    zero = np.zeros((1, 2 * modes), np.float64)
    edge = np.concatenate([real[LOW::LOW], zero, imag[LOW::LOW], zero], axis=0)
    return jnp.asarray(np.concatenate([inner, edge], axis=0), jnp.bfloat16)


def psi_rows(orders):
    order = np.arange(orders, dtype=np.int64)[:, None]
    cos, sin = wave_table(NPSI, np.arange(NPSI, dtype=np.int64)[None, :], order)
    half = np.concatenate([cos, -sin], axis=0)
    return jnp.asarray(np.concatenate([half, half], axis=1), jnp.bfloat16)


def shards(sky_coeffs, beam_coeffs, wigner, visits, point_slot, phi_cell, psi_cell, fraction):
    order_count = lax.axis_size("order")
    shard_count = lax.axis_size("shard")
    local_modes = sky_coeffs.shape[0]
    local_orders = beam_coeffs.shape[0]
    theta_count = wigner.shape[3]
    orders = local_orders * order_count
    modes = local_modes * shard_count
    weighted = (sky_coeffs[:, None, :, :] * beam_coeffs[None, :, None, :]).astype(jnp.bfloat16)
    coeffs = jnp.einsum("mkcl,mklt->mkct", weighted, wigner, preferred_element_type=jnp.float32)
    coeffs = coeffs.astype(jnp.bfloat16).reshape(local_modes * local_orders * 2, theta_count)
    coeffs = pl.pallas_call(
        functools.partial(gather_blocks, shard_count // (SQUARE * CORES)),
        out_shape=jax.ShapeDtypeStruct((shard_count * coeffs.shape[0], theta_count), jnp.bfloat16),
        in_specs=[pl.BlockSpec(memory_space=pltpu.VMEM)],
        out_specs=pl.BlockSpec(memory_space=pltpu.VMEM),
        scratch_shapes=[
            pltpu.SemaphoreType.DMA((shard_count - 1,)),
            pltpu.SemaphoreType.DMA((shard_count,)),
        ],
        compiler_params=pltpu.CompilerParams(collective_id=0, has_side_effects=True),
    )(coeffs)
    if order_count > 1:
        coeffs = coeffs.reshape(modes, local_orders * 2, theta_count)
        coeffs = lax.all_gather(coeffs, "order", axis=1, tiled=True)
        coeffs = coeffs.reshape(modes * orders * 2, theta_count)

    slots = visits.shape[1] * visits.shape[2]
    count = point_slot.shape[0]
    chunks = count // CHUNK
    lined = (chunks, 1, CHUNK)
    pairs = jnp.transpose(fraction.reshape(2, chunks, CHUNK), (1, 0, 2))
    high = PHI_T // LOW
    timeline = pl.pallas_call(
        functools.partial(
            interpolate, modes, orders, order_count, shard_count
        ),
        out_shape=jax.ShapeDtypeStruct(lined, jnp.float32),
        in_specs=[pl.BlockSpec(memory_space=pltpu.VMEM)] * 8,
        out_specs=pl.BlockSpec(memory_space=pltpu.VMEM),
        scratch_shapes=[
            pltpu.VMEM((modes * orders * 2, LANES), jnp.float32),
            pltpu.VMEM((orders * 2 * high, LANES), jnp.float32),
            pltpu.VMEM((orders * 2 * (LOW + 1), high * slots), jnp.bfloat16),
            pltpu.VMEM((orders * 2, CHUNK), jnp.float32),
            pltpu.VMEM((orders * 2, CHUNK), jnp.float32),
            pltpu.VMEM((orders * 2 * (LOW + 1), CHUNK), jnp.float32),
            pltpu.VMEM((orders * 2 * (LOW + 1), CHUNK), jnp.float32),
        ],
    )(
        coeffs,
        jnp.transpose(visits[0]),
        phi_rows(modes),
        psi_rows(orders),
        point_slot.reshape(lined),
        phi_cell.reshape(lined),
        psi_cell.reshape(lined),
        pairs,
    )
    return timeline.reshape(count)


def solution(mesh):
    placed = (
        P("shard", None, None),
        P("order", None),
        P("shard", "order", None, None),
        P(("order", "shard"), None, None),
        P(("order", "shard")),
        P(("order", "shard")),
        P(("order", "shard")),
        P(None, ("order", "shard")),
    )
    return jax.shard_map(
        shards, mesh=mesh, in_specs=placed, out_specs=P(("order", "shard")), check_vma=False
    )
```

```python
import functools
import math

import jax
import jax.numpy as jnp
import numpy as np
from jax import lax
from jax.experimental import pallas as pl
from jax.experimental.pallas import tpu as pltpu
from jax.sharding import PartitionSpec as P

NPHI = 4096
NPSI = 128
PHI_T = 32
LOW = 8
LANES = 128
CHUNK = 256


SQUARE = 4
CORES = 2


def gather_blocks(lines, block_ref, out_ref, send_sem, recv_sem):
    me = lax.axis_index("shard")
    core = me % CORES
    square = me // CORES % SQUARE
    line = me // (CORES * SQUARE)
    depth = block_ref.shape[0]

    def index(at_line, at_square, at_core):
        return (at_line * SQUARE + at_square) * CORES + at_core

    along = [(line + d) % lines for d in range(1, lines)]
    if lines == 4:
        half = line // 2
        along = [line + 1 - 2 * (line % 2), 2 - half, 3 - 3 * half]
    beside, above, corner = square + 1 - 2 * (square % 2), (square + 2) % SQUARE, 3 - square
    other = (core + 1) % CORES
    line_peers = [index(a, square, core) for a in along]
    square_peers = [index(line, b, core) for b in (beside, above)]
    twin = index(line, square, other)
    barrier = pltpu.get_barrier_semaphore()
    peers = line_peers + square_peers + [twin]
    for peer in peers:
        pl.semaphore_signal(
            barrier, inc=1, device_id={"shard": peer}, device_id_type=pl.DeviceIdType.MESH
        )
    pl.semaphore_wait(barrier, len(peers))

    started = []

    def place(owner):
        return out_ref.at[pl.ds(pl.multiple_of(owner * depth, depth), depth), :]

    def send(source, owner, peer):
        copy = pltpu.make_async_remote_copy(
            src_ref=source,
            dst_ref=place(owner),
            send_sem=send_sem.at[len(started)],
            recv_sem=recv_sem.at[owner],
            device_id={"shard": peer},
            device_id_type=pl.DeviceIdType.MESH,
        )
        copy.start()
        started.append(copy)

    def arrive(owner):
        pltpu.make_async_remote_copy(
            src_ref=place(owner),
            dst_ref=place(owner),
            send_sem=send_sem.at[0],
            recv_sem=recv_sem.at[owner],
            device_id={"shard": twin},
            device_id_type=pl.DeviceIdType.MESH,
        ).wait_recv()

    for peer in line_peers[::-1] + square_peers + [twin]:
        send(block_ref, me, peer)
    out_ref[pl.ds(pl.multiple_of(me * depth, depth), depth), :] = block_ref[...]
    for owner in line_peers:
        arrive(owner)
        for peer in square_peers + [twin]:
            send(place(owner), owner, peer)
    for j, a in enumerate([line] + along):
        for b, relayed, peer in (
            (beside, j % 2 == 0, square_peers[1]),
            (above, j % 2 == 1, square_peers[0]),
        ):
            owner = index(a, b, core)
            arrive(owner)
            if relayed:
                send(place(owner), owner, peer)
            send(place(owner), owner, twin)
    for a in [line] + along:
        owner = index(a, corner, core)
        arrive(owner)
        send(place(owner), owner, twin)
    for a in [line] + along:
        for b in (square, beside, above, corner):
            arrive(index(a, b, other))
    for copy in started:
        copy.wait_send()


def wave_table(count, grid, mode):
    phase = 2.0 * math.pi * ((grid * mode) % count) / count
    return np.cos(phase), np.sin(phase)


def interpolate(
    modes,
    orders,
    order_count,
    shard_count,
    coeffs_ref,
    visit_ref,
    phi_table_ref,
    psi_table_ref,
    slot_ref,
    phi_ref,
    psi_ref,
    fraction_ref,
    out_ref,
    picked,
    edge,
    synth,
    wave_a,
    wave_b,
    values_a,
    values_b,
):
    terms = 2 * orders
    high = PHI_T // LOW
    theta = coeffs_ref.shape[1]
    depth, owners = visit_ref.shape
    slots = owners * depth
    blocks = NPHI // (order_count * PHI_T)
    groups = slots // LANES
    listed = jnp.concatenate([visit_ref[d : d + 1, :] for d in range(depth)], axis=1)
    for g in range(groups):
        lanes = slice(g * LANES, (g + 1) * LANES)
        tile = jnp.maximum(listed[:, lanes], 0)
        owner = (lax.broadcasted_iota(jnp.int32, (1, LANES), 1) + g * LANES) % owners
        row = (owner % shard_count) * (theta // shard_count) + tile // blocks
        first_phi = (owner // shard_count) * (NPHI // order_count) + (tile % blocks) * PHI_T
        chosen = (
            lax.broadcasted_iota(jnp.int32, (theta, LANES), 0) == row
        ).astype(jnp.float32).astype(jnp.bfloat16)

        def pick(m, carry):
            rows = pl.ds(pl.multiple_of(m * 4 * terms, 4 * terms), 4 * terms)
            picked[rows, :] = jnp.dot(
                coeffs_ref[rows, :], chosen, preferred_element_type=jnp.float32
            )
            return carry

        lax.fori_loop(0, modes // 4, pick, 0)
        turn = (lax.broadcasted_iota(jnp.int32, (modes, LANES), 0) * first_phi) % NPHI
        angle = turn.astype(jnp.float32) * (2.0 * math.pi / NPHI)
        turn_cos, turn_sin = jnp.cos(angle), jnp.sin(angle)

        def sum_modes(k, carry):
            real = picked[pl.ds(2 * k, modes, stride=terms), :]
            imag = picked[pl.ds(2 * k + 1, modes, stride=terms), :]
            turned = jnp.concatenate(
                [turn_cos * real - turn_sin * imag, turn_sin * real + turn_cos * imag], axis=0
            ).astype(jnp.bfloat16)
            values = jnp.dot(phi_table_ref[...], turned, preferred_element_type=jnp.float32)
            for h in range(high):
                synth[
                    pl.ds(pl.multiple_of(k * 2 * LOW, 2 * LOW), 2 * LOW),
                    h * slots + g * LANES : h * slots + (g + 1) * LANES,
                ] = values[h * 2 * LOW : (h + 1) * 2 * LOW].astype(jnp.bfloat16)
            edge[pl.ds(pl.multiple_of(k * 2 * high, 2 * high), 2 * high), :] = values[
                2 * PHI_T :
            ]
            return carry

        lax.fori_loop(0, orders, sum_modes, 0, unroll=4)
        for part in range(2):
            for h in range(high):
                synth[
                    terms * LOW + part * orders : terms * LOW + (part + 1) * orders,
                    h * slots + g * LANES : h * slots + (g + 1) * LANES,
                ] = edge[pl.ds(part * high + h, orders, stride=2 * high), :].astype(jnp.bfloat16)

    def begin(i, values, wave):
        phi, psi = phi_ref[i], psi_ref[i]
        along_psi = fraction_ref[i][1:2]
        slot = slot_ref[i]
        key = ((phi // LOW) * depth + slot % depth) * owners + slot // depth
        entry = (
            lax.broadcasted_iota(jnp.int32, (high * slots, CHUNK), 0) == key
        ).astype(jnp.float32).astype(jnp.bfloat16)
        at_psi = lax.broadcasted_iota(jnp.int32, (NPSI, CHUNK), 0)
        weight = jnp.where(
            at_psi == psi, 1.0 - along_psi, jnp.where(at_psi == (psi + 1) % NPSI, along_psi, 0.0)
        )
        coarse = weight.astype(jnp.bfloat16)
        fine = (weight - coarse.astype(jnp.float32)).astype(jnp.bfloat16)
        wave[...] = jnp.dot(
            psi_table_ref[...],
            jnp.concatenate([coarse, fine], axis=0),
            preferred_element_type=jnp.float32,
        )
        values[...] = jnp.dot(synth[...], entry, preferred_element_type=jnp.float32)

    def finish(i, values, wave):
        phi = phi_ref[i]
        along_phi = fraction_ref[i][0:1]
        sums = [jnp.zeros((LOW, CHUNK), jnp.float32) for _ in range(4)]
        for k in range(orders):
            for part in range(2):
                at = (2 * k + part) * LOW
                line = part * orders + k
                sums[at // LOW % 4] += values[at : at + LOW, :] * wave[line : line + 1, :]
        inner = (sums[0] + sums[1]) + (sums[2] + sums[3])
        last = jnp.sum(values[terms * LOW :, :] * wave[...], axis=0, keepdims=True)
        low = phi % LOW
        at_low = lax.broadcasted_iota(jnp.int32, (LOW, CHUNK), 0)
        weight_phi = jnp.where(
            at_low == low, 1.0 - along_phi, jnp.where(at_low == low + 1, along_phi, 0.0)
        )
        total = jnp.sum(inner * weight_phi, axis=0, keepdims=True)
        out_ref[i] = total + jnp.where(low == LOW - 1, along_phi, 0.0) * last

    chunks = slot_ref.shape[0]
    begin(0, values_a, wave_a)

    def pair(i, carry):
        begin(2 * i + 1, values_b, wave_b)
        finish(2 * i, values_a, wave_a)
        begin(jnp.minimum(2 * i + 2, chunks - 1), values_a, wave_a)
        finish(2 * i + 1, values_b, wave_b)
        return carry

    lax.fori_loop(0, chunks // 2, pair, 0)


def phi_rows(modes):
    mode = np.arange(modes, dtype=np.int64)[None, :]
    high = PHI_T // LOW
    cos, sin = wave_table(NPHI, np.arange(PHI_T, dtype=np.int64)[:, None], mode)
    real = np.concatenate([cos, -sin], axis=1)
    imag = np.concatenate([sin, cos], axis=1)
    inner = np.stack(
        [real.reshape(high, LOW, 2 * modes), imag.reshape(high, LOW, 2 * modes)], axis=1
    ).reshape(2 * PHI_T, 2 * modes)
    zero = np.zeros((1, 2 * modes), np.float64)
    edge = np.concatenate([real[LOW::LOW], zero, imag[LOW::LOW], zero], axis=0)
    return jnp.asarray(np.concatenate([inner, edge], axis=0), jnp.bfloat16)


def psi_rows(orders):
    order = np.arange(orders, dtype=np.int64)[:, None]
    cos, sin = wave_table(NPSI, np.arange(NPSI, dtype=np.int64)[None, :], order)
    half = np.concatenate([cos, -sin], axis=0)
    return jnp.asarray(np.concatenate([half, half], axis=1), jnp.bfloat16)


def shards(sky_coeffs, beam_coeffs, wigner, visits, point_slot, phi_cell, psi_cell, fraction):
    order_count = lax.axis_size("order")
    shard_count = lax.axis_size("shard")
    local_modes = sky_coeffs.shape[0]
    local_orders = beam_coeffs.shape[0]
    theta_count = wigner.shape[3]
    orders = local_orders * order_count
    modes = local_modes * shard_count
    weighted = (sky_coeffs[:, None, :, :] * beam_coeffs[None, :, None, :]).astype(jnp.bfloat16)
    coeffs = jnp.einsum("mkcl,mklt->mkct", weighted, wigner, preferred_element_type=jnp.float32)
    coeffs = coeffs.astype(jnp.bfloat16).reshape(local_modes * local_orders * 2, theta_count)
    coeffs = pl.pallas_call(
        functools.partial(gather_blocks, shard_count // (SQUARE * CORES)),
        out_shape=jax.ShapeDtypeStruct((shard_count * coeffs.shape[0], theta_count), jnp.bfloat16),
        in_specs=[pl.BlockSpec(memory_space=pltpu.VMEM)],
        out_specs=pl.BlockSpec(memory_space=pltpu.VMEM),
        scratch_shapes=[
            pltpu.SemaphoreType.DMA((shard_count - 1,)),
            pltpu.SemaphoreType.DMA((shard_count,)),
        ],
        compiler_params=pltpu.CompilerParams(collective_id=0, has_side_effects=True),
    )(coeffs)
    if order_count > 1:
        coeffs = coeffs.reshape(modes, local_orders * 2, theta_count)
        coeffs = lax.all_gather(coeffs, "order", axis=1, tiled=True)
        coeffs = coeffs.reshape(modes * orders * 2, theta_count)

    slots = visits.shape[1] * visits.shape[2]
    count = point_slot.shape[0]
    chunks = count // CHUNK
    lined = (chunks, 1, CHUNK)
    pairs = jnp.transpose(fraction.reshape(2, chunks, CHUNK), (1, 0, 2))
    high = PHI_T // LOW
    timeline = pl.pallas_call(
        functools.partial(
            interpolate, modes, orders, order_count, shard_count
        ),
        out_shape=jax.ShapeDtypeStruct(lined, jnp.float32),
        in_specs=[pl.BlockSpec(memory_space=pltpu.VMEM)] * 8,
        out_specs=pl.BlockSpec(memory_space=pltpu.VMEM),
        scratch_shapes=[
            pltpu.VMEM((modes * orders * 2, LANES), jnp.float32),
            pltpu.VMEM((orders * 2 * high, LANES), jnp.float32),
            pltpu.VMEM((orders * 2 * (LOW + 1), high * slots), jnp.bfloat16),
            pltpu.VMEM((orders * 2, CHUNK), jnp.float32),
            pltpu.VMEM((orders * 2, CHUNK), jnp.float32),
            pltpu.VMEM((orders * 2 * (LOW + 1), CHUNK), jnp.float32),
            pltpu.VMEM((orders * 2 * (LOW + 1), CHUNK), jnp.float32),
        ],
    )(
        coeffs,
        jnp.transpose(visits[0]),
        phi_rows(modes),
        psi_rows(orders),
        point_slot.reshape(lined),
        phi_cell.reshape(lined),
        psi_cell.reshape(lined),
        pairs,
    )
    return timeline.reshape(count)


def solution(mesh):
    placed = (
        P("shard", None, None),
        P("order", None),
        P("shard", "order", None, None),
        P(("order", "shard"), None, None),
        P(("order", "shard")),
        P(("order", "shard")),
        P(("order", "shard")),
        P(None, ("order", "shard")),
    )
    return jax.shard_map(
        shards, mesh=mesh, in_specs=placed, out_specs=P(("order", "shard")), check_vma=False
    )
```
